32 devices in a mesh: parts: 2 (over y), gx: 4 (over z), gy: 2 (over x), gz: 2 (over core).
Axes of the slice: x: 2, y: 2, z: 4, core: 2. Of those that a mesh axis runs over, the one named last changes fastest.
Arguments:
- forward_pops: bfloat16 [19, 256, 16, 256], P(None, ('parts', 'gx'), 'gy', 'gz'), parts along dimension 1, as said below
- adjoint_pops: bfloat16 [19, 256, 16, 256], P(None, ('parts', 'gx'), 'gy', 'gz'), parts along dimension 1, may hold values from -6 to 6
- coefficients: float32 [64, 4, 64], P(('parts', 'gx'), 'gy', 'gz'), parts along dimension 0, may hold values from -3 to 3
- node_kind: int32 [256, 16, 256], P(('parts', 'gx'), 'gy', 'gz'), parts along dimension 0, may hold values from 0 to 3, as said below
Outputs:
- prior_adjoint: bfloat16 [19, 256, 16, 256], P(None, ('parts', 'gx'), 'gy', 'gz'), parts along dimension 1
- coef_gradient: float32 [64, 4, 64], P(('parts', 'gx'), 'gy', 'gz'), parts along dimension 0
The draws below stay inside these ranges and needn't reach their ends.
There are 2 independent parts, one for each index of `parts`. The reference program is written for one: setup_inputs(seed, part) draws one part's arguments, and reference() takes and returns one part's arrays. A program takes and returns all parts, laid end to end along the dimension named above; each array names one. Nothing has to cross between parts.
Inputs may be any that keep to these rules, and one draw needn't show every extreme that they name: `node_kind`: node kinds: 0 fluid, 1 solid, 2 inlet, 3 outlet. `forward_pops`: every population lies between 0.4 and 1.7 times the lattice weight of its velocity.
All inputs are finite; a program needn't handle non-finite values.
Results may differ from the reference program's by a relative error of at most 0.001.
Values may be sent and summed in bfloat16 or wider, within the bound.
A program may use at most 64 MiB of HBM per device.

```python
import jax
import jax.numpy as jnp
from jax import lax

CX = 32
NX = 128
NY = 16
NZ = 256
N_GX = 4


WEIGHTS = (1.0 / 3.0,) + (1.0 / 18.0,) * 6 + (1.0 / 36.0,) * 12


EASTWARD = (0.0, 1.0, -1.0, 0.0, 0.0, 0.0, 0.0, 1.0, -1.0, 1.0, -1.0, 1.0, -1.0, 1.0, -1.0, 0.0, 0.0, 0.0, 0.0)


def draw_forward_pops(key, part):
    weights = jnp.array(WEIGHTS, jnp.float32)[:, None, None, None]
    eastward = jnp.array(EASTWARD, jnp.float32)[:, None, None, None]
    noise = jax.random.uniform(key, (19, NX, NY, NZ), jnp.float32, -1.0, 1.0)
    values = weights * (1.0 + 0.15 * eastward + 0.45 * noise)
    return values.astype(jnp.bfloat16)


def draw_node_kind(key, part):
    roll = jax.random.randint(key, (NX, NY, NZ), 0, 20, dtype=jnp.int32)
    return jnp.where(roll < 3, 1, jnp.where(roll == 3, 2, jnp.where(roll == 4, 3, 0))).astype(jnp.int32)


def levels(key, dims, shards, smallest, largest):
    level = 1.0
    for axis_at, parts in shards:
        draws = jax.random.uniform(jax.random.fold_in(jax.random.fold_in(key, 6), axis_at), (parts,), jnp.float32, smallest / len(shards), largest / len(shards))
        level = level * jnp.repeat(jnp.exp(draws), dims[axis_at] // parts).reshape((-1,) + (1,) * (len(dims) - 1 - axis_at))
    return level


def normal_values(own_key, extent, deviation, most, pieces=(), kind=jnp.bfloat16):
    entries = deviation * jax.random.normal(own_key, extent, jnp.float32)
    if pieces:
        entries = entries * levels(own_key, extent, pieces, -0.22, 0.18)
    return jnp.clip(entries, -most, most).astype(kind)


def setup_inputs(seed: int = 0, part: int = 0) -> dict:
    seeds = jax.random.split(jax.random.key(seed), 5)
    part_keys = jax.random.split(jax.random.fold_in(seeds[4], part), 5)
    forward_pops = draw_forward_pops(jax.random.fold_in(jax.random.fold_in(seeds[4], part), 71), part)
    adjoint_pops = normal_values(part_keys[1], (19, NX, NY, NZ), 1.0, 6.0, ((1, 4), (2, 2), (3, 2)))
    coefficients = normal_values(part_keys[2], (NX // 4, NY // 4, NZ // 4), 0.5, 3.0, ((0, 4), (1, 2), (2, 2)), jnp.float32)
    node_kind = draw_node_kind(jax.random.fold_in(jax.random.fold_in(seeds[4], part), 71), part)
    return {"forward_pops": forward_pops, "adjoint_pops": adjoint_pops, "coefficients": coefficients, "node_kind": node_kind}


VELOCITY = ((0, 0, 0), (1, 0, 0), (-1, 0, 0), (0, 1, 0), (0, -1, 0), (0, 0, 1), (0, 0, -1), (1, 1, 0), (-1, -1, 0), (1, -1, 0), (-1, 1, 0), (1, 0, 1), (-1, 0, -1), (1, 0, -1), (-1, 0, 1), (0, 1, 1), (0, -1, -1), (0, 1, -1), (0, -1, 1))
OPPOSITE = (0, 2, 1, 4, 3, 6, 5, 8, 7, 10, 9, 12, 11, 14, 13, 16, 15, 18, 17)
WEIGHTS = (1.0 / 3.0,) + (1.0 / 18.0,) * 6 + (1.0 / 36.0,) * 12
relaxation = 1.6
inlet_speed = 0.05
highest = lax.Precision.HIGHEST

def equilibrium(density, flow_x, flow_y, flow_z):
    square = flow_x * flow_x + flow_y * flow_y + flow_z * flow_z
    layers = []
    for component in range(19):
        step_x, step_y, step_z = VELOCITY[component]
        projection = step_x * flow_x + step_y * flow_y + step_z * flow_z
        layers.append(WEIGHTS[component] * density * (1.0 + 3.0 * projection + 4.5 * projection * projection - 1.5 * square))
    return jnp.stack(layers)

def moment(populations, dimension):
    total = jnp.zeros_like(populations[0])
    for component in range(19):
        factor = VELOCITY[component][dimension]
        if factor != 0:
            total = total + factor * populations[component]
    return total

def collide(populations, porosity, node_kind):
    density = lax.optimization_barrier(jnp.sum(populations, axis=0))
    flow_x = moment(populations, 0) / density
    flow_y = moment(populations, 1) / density
    flow_z = moment(populations, 2) / density
    retained = 1.0 - porosity
    fluid_post = populations - relaxation * (populations - equilibrium(density, retained * flow_x, retained * flow_y, retained * flow_z))
    solid_post = jnp.stack([populations[OPPOSITE[component]] for component in range(19)])
    unit_density = jnp.ones_like(density)
    inlet_post = equilibrium(unit_density, inlet_speed * unit_density, jnp.zeros_like(density), jnp.zeros_like(density))
    outlet_post = equilibrium(unit_density, flow_x, flow_y, flow_z)
    kind_here = node_kind[None]
    return jnp.where(kind_here == 0, fluid_post, jnp.where(kind_here == 1, solid_post, jnp.where(kind_here == 2, inlet_post, outlet_post)))

def basis_matrix(fine_count, coarse_count, fine_offset, coarse_offset):
    fine_pos = jnp.arange(fine_count, dtype=jnp.float32) + fine_offset
    coarse_pos = jnp.arange(coarse_count, dtype=jnp.float32) + coarse_offset
    distance = fine_pos[:, None] - 4.0 * coarse_pos[None, :] - 1.5
    radius = jnp.abs(distance) / 6.0
    return jnp.where(radius < 1.0, (1.0 - radius) ** 4 * (1.0 + 4.0 * radius), 0.0)

def reference(forward_pops, adjoint_pops, coefficients, node_kind):
    basis_x = basis_matrix(NX, NX // 4, 0, 0)
    basis_y = basis_matrix(NY, NY // 4, 0, 0)
    basis_z = basis_matrix(NZ, NZ // 4, 0, 0)
    partway = jnp.einsum('ijk,zk->ijz', coefficients, basis_z, precision=highest)
    partway = jnp.einsum('ijz,yj->iyz', partway, basis_y, precision=highest)
    level_set = jnp.einsum('iyz,xi->xyz', partway, basis_x, precision=highest)
    bent = jnp.tanh(4.0 * level_set)
    porosity = 0.45 * (1.0 - bent)
    slope_phi = -1.8 * (1.0 - bent * bent)
    padded = jnp.pad(adjoint_pops, ((0, 0), (1, 1), (1, 1), (1, 1)))

    def block_step(block_index):
        row_start = (block_index * CX).astype(jnp.int32)
        anchor = jnp.zeros((), jnp.int32)
        piece = lax.dynamic_slice(padded, (anchor, row_start, anchor, anchor), (19, CX + 2, NY + 2, NZ + 2)).astype(jnp.float32)
        pulled = jnp.stack([piece[component, 1 + VELOCITY[component][0]:1 + VELOCITY[component][0] + CX, 1 + VELOCITY[component][1]:1 + VELOCITY[component][1] + NY, 1 + VELOCITY[component][2]:1 + VELOCITY[component][2] + NZ] for component in range(19)])
        forward = lax.dynamic_slice(forward_pops, (anchor, row_start, anchor, anchor), (19, CX, NY, NZ)).astype(jnp.float32)
        local_porosity = lax.dynamic_slice(porosity, (row_start, anchor, anchor), (CX, NY, NZ))
        local_kind = lax.dynamic_slice(node_kind, (row_start, anchor, anchor), (CX, NY, NZ))

        def local_collide(populations, porosity_here):
            return collide(populations, porosity_here, local_kind)
        unused, pullback = jax.vjp(local_collide, forward, local_porosity)
        prior, porosity_bar = pullback(pulled)
        return (prior.astype(jnp.bfloat16), porosity_bar)
    priors, bars = lax.map(block_step, jnp.arange(N_GX, dtype=jnp.int32))
    prior_adjoint = jnp.moveaxis(priors, 1, 0).reshape(19, NX, NY, NZ)
    sensitivity = bars.reshape(NX, NY, NZ) * slope_phi
    gradient = jnp.einsum('xyz,xi->iyz', sensitivity, basis_x, precision=highest)
    gradient = jnp.einsum('iyz,yj->ijz', gradient, basis_y, precision=highest)
    gradient = jnp.einsum('ijz,zk->ijk', gradient, basis_z, precision=highest)
    return (prior_adjoint, gradient)
```

```python
import jax
import jax.numpy as jnp
from jax import lax
from jax.sharding import PartitionSpec as P

VELOCITY = (
    (0, 0, 0),
    (1, 0, 0),
    (-1, 0, 0),
    (0, 1, 0),
    (0, -1, 0),
    (0, 0, 1),
    (0, 0, -1),
    (1, 1, 0),
    (-1, -1, 0),
    (1, -1, 0),
    (-1, 1, 0),
    (1, 0, 1),
    (-1, 0, -1),
    (1, 0, -1),
    (-1, 0, 1),
    (0, 1, 1),
    (0, -1, -1),
    (0, 1, -1),
    (0, -1, 1),
)
OPPOSITE = (0, 2, 1, 4, 3, 6, 5, 8, 7, 10, 9, 12, 11, 14, 13, 16, 15, 18, 17)
WEIGHTS = (1.0 / 3.0,) + (1.0 / 18.0,) * 6 + (1.0 / 36.0,) * 12
relaxation = 1.6
inlet_speed = 0.05
highest = lax.Precision.HIGHEST


def exchange(low_parts, high_parts, axis):
    count = lax.axis_size(axis)
    shapes = [part.shape for part in high_parts]
    types = [part.dtype for part in high_parts]
    sizes = [part.size for part in high_parts]
    wire = jnp.result_type(*types)
    low = jnp.concatenate([part.astype(wire).reshape(-1) for part in low_parts])
    high = jnp.concatenate([part.astype(wire).reshape(-1) for part in high_parts])
    if count == 1:
        from_prev = jnp.zeros_like(high)
        from_next = jnp.zeros_like(low)
    elif count == 2:
        index = lax.axis_index(axis)
        received = lax.ppermute(jnp.where(index == 0, high, low), axis, [(0, 1), (1, 0)])
        from_prev = jnp.where(index == 1, received, jnp.zeros_like(received))
        from_next = jnp.where(index == 0, received, jnp.zeros_like(received))
    else:
        forward = [(i, i + 1) for i in range(count - 1)]
        backward = [(target, source) for source, target in forward]
        from_prev = lax.ppermute(high, axis, forward)
        from_next = lax.ppermute(low, axis, backward)

    def split(flat):
        pieces = []
        offset = 0
        for shape, dtype, size in zip(shapes, types, sizes):
            pieces.append(flat[offset : offset + size].reshape(shape).astype(dtype))
            offset += size
        return pieces

    return split(from_prev), split(from_next)


def faces(block, dim):
    length = block.shape[dim]
    return (
        lax.slice_in_dim(block, 0, 1, axis=dim),
        lax.slice_in_dim(block, length - 1, length, axis=dim),
    )


def padded_pair(coef, coef_dim, pops, pops_dim, axis):
    coef_low, coef_high = faces(coef, coef_dim)
    pops_low, pops_high = faces(pops, pops_dim)
    coef_prev, coef_next = exchange([coef_low], [coef_high], axis)
    pops_prev, pops_next = exchange([pops_low], [pops_high], axis)
    coef = jnp.concatenate([coef_prev[0], coef, coef_next[0]], axis=coef_dim)
    pops = jnp.concatenate([pops_prev[0], pops, pops_next[0]], axis=pops_dim)
    return coef, pops


def equilibrium(density, flow_x, flow_y, flow_z):
    square = flow_x * flow_x + flow_y * flow_y + flow_z * flow_z
    layers = []
    for component in range(19):
        step_x, step_y, step_z = VELOCITY[component]
        projection = step_x * flow_x + step_y * flow_y + step_z * flow_z
        layers.append(
            WEIGHTS[component]
            * density
            * (1.0 + 3.0 * projection + 4.5 * projection * projection - 1.5 * square)
        )
    return jnp.stack(layers)


def moment(populations, dimension):
    total = jnp.zeros_like(populations[0])
    for component in range(19):
        factor = VELOCITY[component][dimension]
        if factor != 0:
            total = total + factor * populations[component]
    return total


def collide(populations, porosity, node_kind):
    density = jnp.sum(populations, axis=0)
    flow_x = moment(populations, 0) / density
    flow_y = moment(populations, 1) / density
    flow_z = moment(populations, 2) / density
    retained = 1.0 - porosity
    fluid_post = populations - relaxation * (
        populations - equilibrium(density, retained * flow_x, retained * flow_y, retained * flow_z)
    )
    solid_post = jnp.stack([populations[OPPOSITE[component]] for component in range(19)])
    unit_density = jnp.ones_like(density)
    inlet_post = equilibrium(
        unit_density, inlet_speed * unit_density, jnp.zeros_like(density), jnp.zeros_like(density)
    )
    outlet_post = equilibrium(unit_density, flow_x, flow_y, flow_z)
    kind_here = node_kind[None]
    return jnp.where(
        kind_here == 0,
        fluid_post,
        jnp.where(kind_here == 1, solid_post, jnp.where(kind_here == 2, inlet_post, outlet_post)),
    )


def basis_matrix(fine_count, coarse_count, fine_offset, coarse_offset):
    fine_pos = jnp.arange(fine_count, dtype=jnp.float32) + fine_offset
    coarse_pos = jnp.arange(coarse_count, dtype=jnp.float32) + coarse_offset
    distance = fine_pos[:, None] - 4.0 * coarse_pos[None, :] - 1.5
    radius = jnp.abs(distance) / 6.0
    return jnp.where(radius < 1.0, (1.0 - radius) ** 4 * (1.0 + 4.0 * radius), 0.0)


def moving(dimension):
    return [component for component in range(19) if VELOCITY[component][dimension] != 0]


def pull_along(lane_list, dimension, extended):
    length_here = lane_list[0].shape[dimension]
    result = list(lane_list)
    for position, component in enumerate(moving(dimension)):
        offset = 1 + VELOCITY[component][dimension]
        result[component] = lax.slice_in_dim(
            extended[position], offset, offset + length_here, axis=dimension
        )
    return result


def fold_rim(partial, dimension, axis):
    length_here = partial.shape[dimension]
    low, high = faces(partial, dimension)
    from_prev, from_next = exchange([low], [high], axis)
    middle = lax.slice_in_dim(partial, 1, length_here - 1, axis=dimension)
    middle_count = length_here - 2
    head_pads = [(0, 0)] * 3
    tail_pads = [(0, 0)] * 3
    head_pads[dimension] = (0, middle_count - 1)
    tail_pads[dimension] = (middle_count - 1, 0)
    return middle + jnp.pad(from_prev[0], head_pads) + jnp.pad(from_next[0], tail_pads)


def per_device(forward_pops, adjoint_pops, coefficients, node_kind):
    cells_x, cells_y, cells_z = node_kind.shape
    coarse_x, coarse_y, coarse_z = coefficients.shape
    basis_x = basis_matrix(cells_x, coarse_x + 2, 0, -1)
    basis_y = basis_matrix(cells_y, coarse_y + 2, 0, -1)
    basis_z = basis_matrix(cells_z, coarse_z + 2, 0, -1)
    lane_list = [adjoint_pops[component] for component in range(19)]
    window = coefficients
    for dimension, axis in ((0, "gx"), (1, "gy"), (2, "gz")):
        stacked = jnp.stack([lane_list[component] for component in moving(dimension)])
        window, extended = padded_pair(window, dimension, stacked, dimension + 1, axis)
        lane_list = pull_along(lane_list, dimension, extended)
    partway = jnp.einsum("ijk,zk->ijz", window, basis_z, precision=highest)
    partway = jnp.einsum("ijz,yj->iyz", partway, basis_y, precision=highest)
    level_set = jnp.einsum("iyz,xi->xyz", partway, basis_x, precision=highest)
    bent = jnp.tanh(4.0 * level_set)
    porosity = 0.45 * (1.0 - bent)
    slope_phi = -1.8 * (1.0 - bent * bent)
    pulled = jnp.stack(lane_list).astype(jnp.float32)
    forward = forward_pops.astype(jnp.float32)

    def local_collide(populations, porosity_here):
        return collide(populations, porosity_here, node_kind)

    unused, pullback = jax.vjp(local_collide, forward, porosity)
    prior, porosity_bar = pullback(pulled)
    prior_adjoint = prior.astype(jnp.bfloat16)
    sensitivity = porosity_bar * slope_phi
    partial_value = jnp.einsum("xyz,xi->iyz", sensitivity, basis_x, precision=highest)
    partial_value = jnp.einsum("iyz,yj->ijz", partial_value, basis_y, precision=highest)
    partial_value = jnp.einsum("ijz,zk->ijk", partial_value, basis_z, precision=highest)
    gradient = fold_rim(fold_rim(fold_rim(partial_value, 0, "gx"), 1, "gy"), 2, "gz")
    return (prior_adjoint, gradient)


def solution(mesh):
    in_specs = (
        P(None, ("parts", "gx"), "gy", "gz"),
        P(None, ("parts", "gx"), "gy", "gz"),
        P(("parts", "gx"), "gy", "gz"),
        P(("parts", "gx"), "gy", "gz"),
    )
    out_specs = (P(None, ("parts", "gx"), "gy", "gz"), P(("parts", "gx"), "gy", "gz"))
    return jax.shard_map(
        per_device, mesh=mesh, in_specs=in_specs, out_specs=out_specs, check_vma=False
    )
```

```python
import jax
import jax.numpy as jnp
from jax import lax
from jax.sharding import PartitionSpec as P

VELOCITY = (
    (0, 0, 0),
    (1, 0, 0),
    (-1, 0, 0),
    (0, 1, 0),
    (0, -1, 0),
    (0, 0, 1),
    (0, 0, -1),
    (1, 1, 0),
    (-1, -1, 0),
    (1, -1, 0),
    (-1, 1, 0),
    (1, 0, 1),
    (-1, 0, -1),
    (1, 0, -1),
    (-1, 0, 1),
    (0, 1, 1),
    (0, -1, -1),
    (0, 1, -1),
    (0, -1, 1),
)
OPPOSITE = (0, 2, 1, 4, 3, 6, 5, 8, 7, 10, 9, 12, 11, 14, 13, 16, 15, 18, 17)
WEIGHTS = (1.0 / 3.0,) + (1.0 / 18.0,) * 6 + (1.0 / 36.0,) * 12
relaxation = 1.6
inlet_speed = 0.05
highest = lax.Precision.HIGHEST


def exchange(low_parts, high_parts, axis):
    count = lax.axis_size(axis)
    if len(high_parts) == 1:
        return exchange_one(low_parts[0], high_parts[0], axis, count)
    shapes = [part.shape for part in high_parts]
    types = [part.dtype for part in high_parts]
    sizes = [part.size for part in high_parts]
    wire = jnp.result_type(*types)
    low = jnp.concatenate([part.astype(wire).reshape(-1) for part in low_parts])
    high = jnp.concatenate([part.astype(wire).reshape(-1) for part in high_parts])
    if count == 1:
        from_prev = jnp.zeros_like(high)
        from_next = jnp.zeros_like(low)
    elif count == 2:
        index = lax.axis_index(axis)
        received = lax.ppermute(jnp.where(index == 0, high, low), axis, [(0, 1), (1, 0)])
        from_prev = jnp.where(index == 1, received, jnp.zeros_like(received))
        from_next = jnp.where(index == 0, received, jnp.zeros_like(received))
    else:
        forward = [(i, i + 1) for i in range(count - 1)]
        backward = [(target, source) for source, target in forward]
        from_prev = lax.ppermute(high, axis, forward)
        from_next = lax.ppermute(low, axis, backward)

    def split(flat):
        pieces = []
        offset = 0
        for shape, dtype, size in zip(shapes, types, sizes):
            pieces.append(flat[offset : offset + size].reshape(shape).astype(dtype))
            offset += size
        return pieces

    return split(from_prev), split(from_next)


def exchange_one(low, high, axis, count):
    if count == 1:
        return [jnp.zeros_like(high)], [jnp.zeros_like(low)]
    if count == 2:
        index = lax.axis_index(axis)
        received = lax.ppermute(jnp.where(index == 0, high, low), axis, [(0, 1), (1, 0)])
        zero = jnp.zeros_like(received)
        return [jnp.where(index == 1, received, zero)], [jnp.where(index == 0, received, zero)]
    forward = [(i, i + 1) for i in range(count - 1)]
    backward = [(target, source) for source, target in forward]
    return [lax.ppermute(high, axis, forward)], [lax.ppermute(low, axis, backward)]


def faces(block, dim):
    length = block.shape[dim]
    return (
        lax.slice_in_dim(block, 0, 1, axis=dim),
        lax.slice_in_dim(block, length - 1, length, axis=dim),
    )


def padded_pair(coef, coef_dim, pops, pops_dim, axis):
    coef_low, coef_high = faces(coef, coef_dim)
    pops_low, pops_high = faces(pops, pops_dim)
    coef_prev, coef_next = exchange([coef_low], [coef_high], axis)
    pops_prev, pops_next = exchange([pops_low], [pops_high], axis)
    coef = jnp.concatenate([coef_prev[0], coef, coef_next[0]], axis=coef_dim)
    pops = jnp.concatenate([pops_prev[0], pops, pops_next[0]], axis=pops_dim)
    return coef, pops


def equilibrium(density, flow_x, flow_y, flow_z):
    square = flow_x * flow_x + flow_y * flow_y + flow_z * flow_z
    layers = []
    for component in range(19):
        step_x, step_y, step_z = VELOCITY[component]
        projection = step_x * flow_x + step_y * flow_y + step_z * flow_z
        layers.append(
            WEIGHTS[component]
            * density
            * (1.0 + 3.0 * projection + 4.5 * projection * projection - 1.5 * square)
        )
    return jnp.stack(layers)


def moment(populations, dimension):
    total = jnp.zeros_like(populations[0])
    for component in range(19):
        factor = VELOCITY[component][dimension]
        if factor != 0:
            total = total + factor * populations[component]
    return total


def collide(populations, porosity, node_kind):
    density = jnp.sum(populations, axis=0)
    flow_x = moment(populations, 0) / density
    flow_y = moment(populations, 1) / density
    flow_z = moment(populations, 2) / density
    retained = 1.0 - porosity
    fluid_post = populations - relaxation * (
        populations - equilibrium(density, retained * flow_x, retained * flow_y, retained * flow_z)
    )
    solid_post = jnp.stack([populations[OPPOSITE[component]] for component in range(19)])
    unit_density = jnp.ones_like(density)
    inlet_post = equilibrium(
        unit_density, inlet_speed * unit_density, jnp.zeros_like(density), jnp.zeros_like(density)
    )
    outlet_post = equilibrium(unit_density, flow_x, flow_y, flow_z)
    kind_here = node_kind[None]
    return jnp.where(
        kind_here == 0,
        fluid_post,
        jnp.where(kind_here == 1, solid_post, jnp.where(kind_here == 2, inlet_post, outlet_post)),
    )


def basis_matrix(fine_count, coarse_count, fine_offset, coarse_offset):
    fine_pos = jnp.arange(fine_count, dtype=jnp.float32) + fine_offset
    coarse_pos = jnp.arange(coarse_count, dtype=jnp.float32) + coarse_offset
    distance = fine_pos[:, None] - 4.0 * coarse_pos[None, :] - 1.5
    radius = jnp.abs(distance) / 6.0
    return jnp.where(radius < 1.0, (1.0 - radius) ** 4 * (1.0 + 4.0 * radius), 0.0)


def moving(dimension):
    return [component for component in range(19) if VELOCITY[component][dimension] != 0]


def pull_along(lane_list, dimension, extended):
    length_here = lane_list[0].shape[dimension]
    result = list(lane_list)
    for position, component in enumerate(moving(dimension)):
        offset = 1 + VELOCITY[component][dimension]
        result[component] = lax.slice_in_dim(
            extended[position], offset, offset + length_here, axis=dimension
        )
    return result


def fold_rim(partial, dimension, axis):
    length_here = partial.shape[dimension]
    low, high = faces(partial, dimension)
    from_prev, from_next = exchange([low], [high], axis)
    middle = lax.slice_in_dim(partial, 1, length_here - 1, axis=dimension)
    middle_count = length_here - 2
    head_pads = [(0, 0)] * 3
    tail_pads = [(0, 0)] * 3
    head_pads[dimension] = (0, middle_count - 1)
    tail_pads[dimension] = (middle_count - 1, 0)
    return middle + jnp.pad(from_prev[0], head_pads) + jnp.pad(from_next[0], tail_pads)


def per_device(forward_pops, adjoint_pops, coefficients, node_kind):
    cells_x, cells_y, cells_z = node_kind.shape
    coarse_x, coarse_y, coarse_z = coefficients.shape
    basis_x = basis_matrix(cells_x, coarse_x + 2, 0, -1)
    basis_y = basis_matrix(cells_y, coarse_y + 2, 0, -1)
    basis_z = basis_matrix(cells_z, coarse_z + 2, 0, -1)
    window = coefficients
    extended = adjoint_pops
    for dimension, axis in ((0, "gx"), (1, "gy"), (2, "gz")):
        coef_low, coef_high = faces(window, dimension)
        coef_prev, coef_next = exchange([coef_low], [coef_high], axis)
        window = jnp.concatenate([coef_prev[0], window, coef_next[0]], axis=dimension)
        pops_low, pops_high = faces(extended, dimension + 1)
        pops_prev, pops_next = exchange([pops_low], [pops_high], axis)
        extended = jnp.concatenate([pops_prev[0], extended, pops_next[0]], axis=dimension + 1)
    lane_list = []
    for component in range(19):
        step_x, step_y, step_z = VELOCITY[component]
        lane_list.append(
            extended[
                component,
                1 + step_x : 1 + step_x + cells_x,
                1 + step_y : 1 + step_y + cells_y,
                1 + step_z : 1 + step_z + cells_z,
            ]
        )
    partway = jnp.einsum("ijk,zk->ijz", window, basis_z, precision=highest)
    partway = jnp.einsum("ijz,yj->iyz", partway, basis_y, precision=highest)
    level_set = jnp.einsum("iyz,xi->xyz", partway, basis_x, precision=highest)
    bent = jnp.tanh(4.0 * level_set)
    porosity = 0.45 * (1.0 - bent)
    slope_phi = -1.8 * (1.0 - bent * bent)
    pulled = jnp.stack(lane_list).astype(jnp.float32)
    forward = forward_pops.astype(jnp.float32)

    def local_collide(populations, porosity_here):
        return collide(populations, porosity_here, node_kind)

    unused, pullback = jax.vjp(local_collide, forward, porosity)
    prior, porosity_bar = pullback(pulled)
    prior_adjoint = prior.astype(jnp.bfloat16)
    sensitivity = porosity_bar * slope_phi
    partial_value = jnp.einsum("xyz,xi->iyz", sensitivity, basis_x, precision=highest)
    partial_value = jnp.einsum("iyz,yj->ijz", partial_value, basis_y, precision=highest)
    partial_value = jnp.einsum("ijz,zk->ijk", partial_value, basis_z, precision=highest)
    gradient = fold_rim(fold_rim(fold_rim(partial_value, 0, "gx"), 1, "gy"), 2, "gz")
    return (prior_adjoint, gradient)


def solution(mesh):
    in_specs = (
        P(None, ("parts", "gx"), "gy", "gz"),
        P(None, ("parts", "gx"), "gy", "gz"),
        P(("parts", "gx"), "gy", "gz"),
        P(("parts", "gx"), "gy", "gz"),
    )
    out_specs = (P(None, ("parts", "gx"), "gy", "gz"), P(("parts", "gx"), "gy", "gz"))
    return jax.shard_map(
        per_device, mesh=mesh, in_specs=in_specs, out_specs=out_specs, check_vma=False
    )
```

```python
import jax
import jax.numpy as jnp
from jax import lax
from jax.sharding import PartitionSpec as P

VELOCITY = (
    (0, 0, 0),
    (1, 0, 0),
    (-1, 0, 0),
    (0, 1, 0),
    (0, -1, 0),
    (0, 0, 1),
    (0, 0, -1),
    (1, 1, 0),
    (-1, -1, 0),
    (1, -1, 0),
    (-1, 1, 0),
    (1, 0, 1),
    (-1, 0, -1),
    (1, 0, -1),
    (-1, 0, 1),
    (0, 1, 1),
    (0, -1, -1),
    (0, 1, -1),
    (0, -1, 1),
)
OPPOSITE = (0, 2, 1, 4, 3, 6, 5, 8, 7, 10, 9, 12, 11, 14, 13, 16, 15, 18, 17)
WEIGHTS = (1.0 / 3.0,) + (1.0 / 18.0,) * 6 + (1.0 / 36.0,) * 12
relaxation = 1.6
inlet_speed = 0.05
highest = lax.Precision.HIGHEST


def exchange_one(low, high, axis, count):
    if count == 1:
        return [jnp.zeros_like(high)], [jnp.zeros_like(low)]
    if count == 2:
        index = lax.axis_index(axis)
        received = lax.ppermute(jnp.where(index == 0, high, low), axis, [(0, 1), (1, 0)])
        zero = jnp.zeros_like(received)
        return [jnp.where(index == 1, received, zero)], [jnp.where(index == 0, received, zero)]
    forward = [(i, i + 1) for i in range(count - 1)]
    backward = [(target, source) for source, target in forward]
    return [lax.ppermute(high, axis, forward)], [lax.ppermute(low, axis, backward)]


def padded_swap(block, sides):
    for axis, dim in sides:
        length = block.shape[dim]
        low = lax.slice_in_dim(block, 0, 1, axis=dim)
        high = lax.slice_in_dim(block, length - 1, length, axis=dim)
        from_prev, from_next = exchange_one(low, high, axis, lax.axis_size(axis))
        block = jnp.concatenate([from_prev[0], block, from_next[0]], axis=dim)
    return block


def padded(block, sides, width):
    for axis, dim in sides:
        count = lax.axis_size(axis)
        forward = [(i, i + 1) for i in range(count - 1)]
        backward = [(target, source) for source, target in forward]
        low = lax.ppermute(
            lax.slice_in_dim(block, block.shape[dim] - width, None, axis=dim), axis, forward
        )
        high = lax.ppermute(lax.slice_in_dim(block, 0, width, axis=dim), axis, backward)
        block = jnp.concatenate([low, block, high], axis=dim)
    return block


def equilibrium(density, flow_x, flow_y, flow_z):
    square = flow_x * flow_x + flow_y * flow_y + flow_z * flow_z
    layers = []
    for component in range(19):
        step_x, step_y, step_z = VELOCITY[component]
        projection = step_x * flow_x + step_y * flow_y + step_z * flow_z
        layers.append(
            WEIGHTS[component]
            * density
            * (1.0 + 3.0 * projection + 4.5 * projection * projection - 1.5 * square)
        )
    return jnp.stack(layers)


def moment(populations, dimension):
    total = jnp.zeros_like(populations[0])
    for component in range(19):
        factor = VELOCITY[component][dimension]
        if factor != 0:
            total = total + factor * populations[component]
    return total


def collide(populations, porosity, node_kind):
    density = jnp.sum(populations, axis=0)
    flow_x = moment(populations, 0) / density
    flow_y = moment(populations, 1) / density
    flow_z = moment(populations, 2) / density
    retained = 1.0 - porosity
    fluid_post = populations - relaxation * (
        populations - equilibrium(density, retained * flow_x, retained * flow_y, retained * flow_z)
    )
    solid_post = jnp.stack([populations[OPPOSITE[component]] for component in range(19)])
    unit_density = jnp.ones_like(density)
    inlet_post = equilibrium(
        unit_density, inlet_speed * unit_density, jnp.zeros_like(density), jnp.zeros_like(density)
    )
    outlet_post = equilibrium(unit_density, flow_x, flow_y, flow_z)
    kind_here = node_kind[None]
    return jnp.where(
        kind_here == 0,
        fluid_post,
        jnp.where(kind_here == 1, solid_post, jnp.where(kind_here == 2, inlet_post, outlet_post)),
    )


def basis_matrix(fine_count, coarse_count, fine_offset, coarse_offset):
    fine_pos = jnp.arange(fine_count, dtype=jnp.float32) + fine_offset
    coarse_pos = jnp.arange(coarse_count, dtype=jnp.float32) + coarse_offset
    distance = fine_pos[:, None] - 4.0 * coarse_pos[None, :] - 1.5
    radius = jnp.abs(distance) / 6.0
    return jnp.where(radius < 1.0, (1.0 - radius) ** 4 * (1.0 + 4.0 * radius), 0.0)


def moving(dimension):
    return [component for component in range(19) if VELOCITY[component][dimension] != 0]


def pull_along(lane_list, dimension, extended):
    length_here = lane_list[0].shape[dimension]
    result = list(lane_list)
    for position, component in enumerate(moving(dimension)):
        offset = 1 + VELOCITY[component][dimension]
        result[component] = lax.slice_in_dim(
            extended[position], offset, offset + length_here, axis=dimension
        )
    return result


def fold_rim(bordered, dimension):
    length_here = bordered.shape[dimension]
    middle = lax.slice_in_dim(bordered, 2, length_here - 2, axis=dimension)
    head_slice = lax.slice_in_dim(bordered, 0, 1, axis=dimension)
    tail_slice = lax.slice_in_dim(bordered, length_here - 1, length_here, axis=dimension)
    middle_count = length_here - 4
    head_pads = [(0, 0)] * 3
    tail_pads = [(0, 0)] * 3
    head_pads[dimension] = (0, middle_count - 1)
    tail_pads[dimension] = (middle_count - 1, 0)
    return middle + jnp.pad(head_slice, head_pads) + jnp.pad(tail_slice, tail_pads)


def per_device(forward_pops, adjoint_pops, coefficients, node_kind):
    cells_x, cells_y, cells_z = node_kind.shape
    coarse_x, coarse_y, coarse_z = coefficients.shape
    window = padded_swap(coefficients, (("gx", 0), ("gy", 1), ("gz", 2)))
    basis_x = basis_matrix(cells_x, coarse_x + 2, 0, -1)
    basis_y = basis_matrix(cells_y, coarse_y + 2, 0, -1)
    basis_z = basis_matrix(cells_z, coarse_z + 2, 0, -1)
    partway = jnp.einsum("ijk,zk->ijz", window, basis_z, precision=highest)
    partway = jnp.einsum("ijz,yj->iyz", partway, basis_y, precision=highest)
    level_set = jnp.einsum("iyz,xi->xyz", partway, basis_x, precision=highest)
    bent = jnp.tanh(4.0 * level_set)
    porosity = 0.45 * (1.0 - bent)
    slope_phi = -1.8 * (1.0 - bent * bent)
    lane_list = [adjoint_pops[component] for component in range(19)]
    extended = padded(jnp.stack([lane_list[component] for component in moving(0)]), (("gx", 1),), 1)
    lane_list = pull_along(lane_list, 0, extended)
    extended = padded(jnp.stack([lane_list[component] for component in moving(1)]), (("gy", 2),), 1)
    lane_list = pull_along(lane_list, 1, extended)
    extended = padded(jnp.stack([lane_list[component] for component in moving(2)]), (("gz", 3),), 1)
    lane_list = pull_along(lane_list, 2, extended)
    pulled = jnp.stack(lane_list).astype(jnp.float32)
    forward = forward_pops.astype(jnp.float32)

    def local_collide(populations, porosity_here):
        return collide(populations, porosity_here, node_kind)

    unused, pullback = jax.vjp(local_collide, forward, porosity)
    prior, porosity_bar = pullback(pulled)
    prior_adjoint = prior.astype(jnp.bfloat16)
    sensitivity = porosity_bar * slope_phi
    partial_value = jnp.einsum("xyz,xi->iyz", sensitivity, basis_x, precision=highest)
    partial_value = jnp.einsum("iyz,yj->ijz", partial_value, basis_y, precision=highest)
    partial_value = jnp.einsum("ijz,zk->ijk", partial_value, basis_z, precision=highest)
    bordered = padded_swap(partial_value, (("gx", 0), ("gy", 1), ("gz", 2)))
    gradient = fold_rim(fold_rim(fold_rim(bordered, 0), 1), 2)
    return (prior_adjoint, gradient)


def solution(mesh):
    in_specs = (
        P(None, ("parts", "gx"), "gy", "gz"),
        P(None, ("parts", "gx"), "gy", "gz"),
        P(("parts", "gx"), "gy", "gz"),
        P(("parts", "gx"), "gy", "gz"),
    )
    out_specs = (P(None, ("parts", "gx"), "gy", "gz"), P(("parts", "gx"), "gy", "gz"))
    return jax.shard_map(
        per_device, mesh=mesh, in_specs=in_specs, out_specs=out_specs, check_vma=False
    )
```

```python
import jax
import jax.numpy as jnp
from jax import lax
from jax.sharding import PartitionSpec as P

VELOCITY = (
    (0, 0, 0),
    (1, 0, 0),
    (-1, 0, 0),
    (0, 1, 0),
    (0, -1, 0),
    (0, 0, 1),
    (0, 0, -1),
    (1, 1, 0),
    (-1, -1, 0),
    (1, -1, 0),
    (-1, 1, 0),
    (1, 0, 1),
    (-1, 0, -1),
    (1, 0, -1),
    (-1, 0, 1),
    (0, 1, 1),
    (0, -1, -1),
    (0, 1, -1),
    (0, -1, 1),
)
OPPOSITE = (0, 2, 1, 4, 3, 6, 5, 8, 7, 10, 9, 12, 11, 14, 13, 16, 15, 18, 17)
WEIGHTS = (1.0 / 3.0,) + (1.0 / 18.0,) * 6 + (1.0 / 36.0,) * 12
relaxation = 1.6
inlet_speed = 0.05
highest = lax.Precision.HIGHEST


def padded(block, sides, width):
    for axis, dim in sides:
        count = lax.axis_size(axis)
        forward = [(i, i + 1) for i in range(count - 1)]
        backward = [(target, source) for source, target in forward]
        low = lax.ppermute(
            lax.slice_in_dim(block, block.shape[dim] - width, None, axis=dim), axis, forward
        )
        high = lax.ppermute(lax.slice_in_dim(block, 0, width, axis=dim), axis, backward)
        block = jnp.concatenate([low, block, high], axis=dim)
    return block


def equilibrium(density, flow_x, flow_y, flow_z):
    square = flow_x * flow_x + flow_y * flow_y + flow_z * flow_z
    layers = []
    for component in range(19):
        step_x, step_y, step_z = VELOCITY[component]
        projection = step_x * flow_x + step_y * flow_y + step_z * flow_z
        layers.append(
            WEIGHTS[component]
            * density
            * (1.0 + 3.0 * projection + 4.5 * projection * projection - 1.5 * square)
        )
    return jnp.stack(layers)


def moment(populations, dimension):
    total = jnp.zeros_like(populations[0])
    for component in range(19):
        factor = VELOCITY[component][dimension]
        if factor != 0:
            total = total + factor * populations[component]
    return total


def collide(populations, porosity, node_kind):
    density = jnp.sum(populations, axis=0)
    flow_x = moment(populations, 0) / density
    flow_y = moment(populations, 1) / density
    flow_z = moment(populations, 2) / density
    retained = 1.0 - porosity
    fluid_post = populations - relaxation * (
        populations - equilibrium(density, retained * flow_x, retained * flow_y, retained * flow_z)
    )
    solid_post = jnp.stack([populations[OPPOSITE[component]] for component in range(19)])
    unit_density = jnp.ones_like(density)
    inlet_post = equilibrium(
        unit_density, inlet_speed * unit_density, jnp.zeros_like(density), jnp.zeros_like(density)
    )
    outlet_post = equilibrium(unit_density, flow_x, flow_y, flow_z)
    kind_here = node_kind[None]
    return jnp.where(
        kind_here == 0,
        fluid_post,
        jnp.where(kind_here == 1, solid_post, jnp.where(kind_here == 2, inlet_post, outlet_post)),
    )


def basis_matrix(fine_count, coarse_count, fine_offset, coarse_offset):
    fine_pos = jnp.arange(fine_count, dtype=jnp.float32) + fine_offset
    coarse_pos = jnp.arange(coarse_count, dtype=jnp.float32) + coarse_offset
    distance = fine_pos[:, None] - 4.0 * coarse_pos[None, :] - 1.5
    radius = jnp.abs(distance) / 6.0
    return jnp.where(radius < 1.0, (1.0 - radius) ** 4 * (1.0 + 4.0 * radius), 0.0)


def moving(dimension):
    return [component for component in range(19) if VELOCITY[component][dimension] != 0]


def pull_along(lane_list, dimension, extended):
    length_here = lane_list[0].shape[dimension]
    result = list(lane_list)
    for position, component in enumerate(moving(dimension)):
        offset = 1 + VELOCITY[component][dimension]
        result[component] = lax.slice_in_dim(
            extended[position], offset, offset + length_here, axis=dimension
        )
    return result


def fold_rim(bordered, dimension):
    length_here = bordered.shape[dimension]
    middle = lax.slice_in_dim(bordered, 2, length_here - 2, axis=dimension)
    head_slice = lax.slice_in_dim(bordered, 0, 1, axis=dimension)
    tail_slice = lax.slice_in_dim(bordered, length_here - 1, length_here, axis=dimension)
    middle_count = length_here - 4
    head_pads = [(0, 0)] * 3
    tail_pads = [(0, 0)] * 3
    head_pads[dimension] = (0, middle_count - 1)
    tail_pads[dimension] = (middle_count - 1, 0)
    return middle + jnp.pad(head_slice, head_pads) + jnp.pad(tail_slice, tail_pads)


def per_device(forward_pops, adjoint_pops, coefficients, node_kind):
    cells_x, cells_y, cells_z = node_kind.shape
    coarse_x, coarse_y, coarse_z = coefficients.shape
    count_x, count_y, count_z = (lax.axis_size(axis) for axis in ("gx", "gy", "gz"))
    gathered = lax.all_gather(coefficients, ("gx", "gy", "gz"))
    gathered = gathered.reshape(count_x, count_y, count_z, coarse_x, coarse_y, coarse_z)
    gathered = gathered.transpose(0, 3, 1, 4, 2, 5).reshape(
        count_x * coarse_x, count_y * coarse_y, count_z * coarse_z
    )
    start_x, start_y, start_z = (
        (lax.axis_index(axis) * cells).astype(jnp.float32)
        for axis, cells in (("gx", cells_x), ("gy", cells_y), ("gz", cells_z))
    )
    full_x = basis_matrix(cells_x, count_x * coarse_x, start_x, 0)
    full_y = basis_matrix(cells_y, count_y * coarse_y, start_y, 0)
    full_z = basis_matrix(cells_z, count_z * coarse_z, start_z, 0)
    partway = jnp.einsum("ijk,zk->ijz", gathered, full_z, precision=highest)
    partway = jnp.einsum("ijz,yj->iyz", partway, full_y, precision=highest)
    level_set = jnp.einsum("iyz,xi->xyz", partway, full_x, precision=highest)
    basis_x = basis_matrix(cells_x, coarse_x + 2, 0, -1)
    basis_y = basis_matrix(cells_y, coarse_y + 2, 0, -1)
    basis_z = basis_matrix(cells_z, coarse_z + 2, 0, -1)
    bent = jnp.tanh(4.0 * level_set)
    porosity = 0.45 * (1.0 - bent)
    slope_phi = -1.8 * (1.0 - bent * bent)
    lane_list = [adjoint_pops[component] for component in range(19)]
    extended = padded(jnp.stack([lane_list[component] for component in moving(0)]), (("gx", 1),), 1)
    lane_list = pull_along(lane_list, 0, extended)
    extended = padded(jnp.stack([lane_list[component] for component in moving(1)]), (("gy", 2),), 1)
    lane_list = pull_along(lane_list, 1, extended)
    extended = padded(jnp.stack([lane_list[component] for component in moving(2)]), (("gz", 3),), 1)
    lane_list = pull_along(lane_list, 2, extended)
    pulled = jnp.stack(lane_list).astype(jnp.float32)
    forward = forward_pops.astype(jnp.float32)

    def local_collide(populations, porosity_here):
        return collide(populations, porosity_here, node_kind)

    unused, pullback = jax.vjp(local_collide, forward, porosity)
    prior, porosity_bar = pullback(pulled)
    prior_adjoint = prior.astype(jnp.bfloat16)
    sensitivity = porosity_bar * slope_phi
    partial_value = jnp.einsum("xyz,xi->iyz", sensitivity, basis_x, precision=highest)
    partial_value = jnp.einsum("iyz,yj->ijz", partial_value, basis_y, precision=highest)
    partial_value = jnp.einsum("ijz,zk->ijk", partial_value, basis_z, precision=highest)
    bordered = padded(partial_value, (("gx", 0), ("gy", 1), ("gz", 2)), 1)
    gradient = fold_rim(fold_rim(fold_rim(bordered, 0), 1), 2)
    return (prior_adjoint, gradient)


def solution(mesh):
    in_specs = (
        P(None, ("parts", "gx"), "gy", "gz"),
        P(None, ("parts", "gx"), "gy", "gz"),
        P(("parts", "gx"), "gy", "gz"),
        P(("parts", "gx"), "gy", "gz"),
    )
    out_specs = (P(None, ("parts", "gx"), "gy", "gz"), P(("parts", "gx"), "gy", "gz"))
    return jax.shard_map(
        per_device, mesh=mesh, in_specs=in_specs, out_specs=out_specs, check_vma=False
    )
```

```python
import jax
import jax.numpy as jnp
from jax import lax
from jax.sharding import PartitionSpec as P

VELOCITY = (
    (0, 0, 0),
    (1, 0, 0),
    (-1, 0, 0),
    (0, 1, 0),
    (0, -1, 0),
    (0, 0, 1),
    (0, 0, -1),
    (1, 1, 0),
    (-1, -1, 0),
    (1, -1, 0),
    (-1, 1, 0),
    (1, 0, 1),
    (-1, 0, -1),
    (1, 0, -1),
    (-1, 0, 1),
    (0, 1, 1),
    (0, -1, -1),
    (0, 1, -1),
    (0, -1, 1),
)
OPPOSITE = (0, 2, 1, 4, 3, 6, 5, 8, 7, 10, 9, 12, 11, 14, 13, 16, 15, 18, 17)
WEIGHTS = (1.0 / 3.0,) + (1.0 / 18.0,) * 6 + (1.0 / 36.0,) * 12
relaxation = 1.6
inlet_speed = 0.05
highest = lax.Precision.HIGHEST


def padded(block, sides, width):
    for axis, dim in sides:
        count = lax.axis_size(axis)
        forward = [(i, i + 1) for i in range(count - 1)]
        backward = [(target, source) for source, target in forward]
        low = lax.ppermute(
            lax.slice_in_dim(block, block.shape[dim] - width, None, axis=dim), axis, forward
        )
        high = lax.ppermute(lax.slice_in_dim(block, 0, width, axis=dim), axis, backward)
        block = jnp.concatenate([low, block, high], axis=dim)
    return block


def equilibrium(density, flow_x, flow_y, flow_z):
    square = flow_x * flow_x + flow_y * flow_y + flow_z * flow_z
    layers = []
    for component in range(19):
        step_x, step_y, step_z = VELOCITY[component]
        projection = step_x * flow_x + step_y * flow_y + step_z * flow_z
        layers.append(
            WEIGHTS[component]
            * density
            * (1.0 + 3.0 * projection + 4.5 * projection * projection - 1.5 * square)
        )
    return jnp.stack(layers)


def moment(populations, dimension):
    total = jnp.zeros_like(populations[0])
    for component in range(19):
        factor = VELOCITY[component][dimension]
        if factor != 0:
            total = total + factor * populations[component]
    return total


def collide(populations, porosity, node_kind):
    density = jnp.sum(populations, axis=0)
    flow_x = moment(populations, 0) / density
    flow_y = moment(populations, 1) / density
    flow_z = moment(populations, 2) / density
    retained = 1.0 - porosity
    fluid_post = populations - relaxation * (
        populations - equilibrium(density, retained * flow_x, retained * flow_y, retained * flow_z)
    )
    solid_post = jnp.stack([populations[OPPOSITE[component]] for component in range(19)])
    unit_density = jnp.ones_like(density)
    inlet_post = equilibrium(
        unit_density, inlet_speed * unit_density, jnp.zeros_like(density), jnp.zeros_like(density)
    )
    outlet_post = equilibrium(unit_density, flow_x, flow_y, flow_z)
    kind_here = node_kind[None]
    return jnp.where(
        kind_here == 0,
        fluid_post,
        jnp.where(kind_here == 1, solid_post, jnp.where(kind_here == 2, inlet_post, outlet_post)),
    )


def basis_matrix(fine_count, coarse_count, fine_offset, coarse_offset):
    fine_pos = jnp.arange(fine_count, dtype=jnp.float32) + fine_offset
    coarse_pos = jnp.arange(coarse_count, dtype=jnp.float32) + coarse_offset
    distance = fine_pos[:, None] - 4.0 * coarse_pos[None, :] - 1.5
    radius = jnp.abs(distance) / 6.0
    return jnp.where(radius < 1.0, (1.0 - radius) ** 4 * (1.0 + 4.0 * radius), 0.0)


def moving(dimension):
    return [component for component in range(19) if VELOCITY[component][dimension] != 0]


def pull_along(lane_list, dimension, extended):
    length_here = lane_list[0].shape[dimension]
    result = list(lane_list)
    for position, component in enumerate(moving(dimension)):
        offset = 1 + VELOCITY[component][dimension]
        result[component] = lax.slice_in_dim(
            extended[position], offset, offset + length_here, axis=dimension
        )
    return result


def fold_rim(bordered, dimension):
    length_here = bordered.shape[dimension]
    middle = lax.slice_in_dim(bordered, 2, length_here - 2, axis=dimension)
    head_slice = lax.slice_in_dim(bordered, 0, 1, axis=dimension)
    tail_slice = lax.slice_in_dim(bordered, length_here - 1, length_here, axis=dimension)
    middle_count = length_here - 4
    head_pads = [(0, 0)] * 3
    tail_pads = [(0, 0)] * 3
    head_pads[dimension] = (0, middle_count - 1)
    tail_pads[dimension] = (middle_count - 1, 0)
    return middle + jnp.pad(head_slice, head_pads) + jnp.pad(tail_slice, tail_pads)


def per_device(forward_pops, adjoint_pops, coefficients, node_kind):
    cells_x, cells_y, cells_z = node_kind.shape
    coarse_x, coarse_y, coarse_z = coefficients.shape
    lane_list = [adjoint_pops[component] for component in range(19)]
    window = coefficients
    for dimension, axis in ((0, "gx"), (1, "gy"), (2, "gz")):
        stacked = jnp.stack([lane_list[component] for component in moving(dimension)])
        window, stacked = lax.optimization_barrier((window, stacked))
        window = padded(window, ((axis, dimension),), 1)
        extended = padded(stacked, ((axis, dimension + 1),), 1)
        window, extended = lax.optimization_barrier((window, extended))
        lane_list = pull_along(lane_list, dimension, extended)
    basis_x = basis_matrix(cells_x, coarse_x + 2, 0, -1)
    basis_y = basis_matrix(cells_y, coarse_y + 2, 0, -1)
    basis_z = basis_matrix(cells_z, coarse_z + 2, 0, -1)
    partway = jnp.einsum("ijk,zk->ijz", window, basis_z, precision=highest)
    partway = jnp.einsum("ijz,yj->iyz", partway, basis_y, precision=highest)
    level_set = jnp.einsum("iyz,xi->xyz", partway, basis_x, precision=highest)
    bent = jnp.tanh(4.0 * level_set)
    porosity = 0.45 * (1.0 - bent)
    slope_phi = -1.8 * (1.0 - bent * bent)
    pulled = jnp.stack(lane_list).astype(jnp.float32)
    forward = forward_pops.astype(jnp.float32)

    def local_collide(populations, porosity_here):
        return collide(populations, porosity_here, node_kind)

    unused, pullback = jax.vjp(local_collide, forward, porosity)
    prior, porosity_bar = pullback(pulled)
    prior_adjoint = prior.astype(jnp.bfloat16)
    sensitivity = porosity_bar * slope_phi
    partial_value = jnp.einsum("xyz,xi->iyz", sensitivity, basis_x, precision=highest)
    partial_value = jnp.einsum("iyz,yj->ijz", partial_value, basis_y, precision=highest)
    partial_value = jnp.einsum("ijz,zk->ijk", partial_value, basis_z, precision=highest)
    bordered = padded(partial_value, (("gx", 0), ("gy", 1), ("gz", 2)), 1)
    gradient = fold_rim(fold_rim(fold_rim(bordered, 0), 1), 2)
    return (prior_adjoint, gradient)


def solution(mesh):
    in_specs = (
        P(None, ("parts", "gx"), "gy", "gz"),
        P(None, ("parts", "gx"), "gy", "gz"),
        P(("parts", "gx"), "gy", "gz"),
        P(("parts", "gx"), "gy", "gz"),
    )
    out_specs = (P(None, ("parts", "gx"), "gy", "gz"), P(("parts", "gx"), "gy", "gz"))
    return jax.shard_map(
        per_device, mesh=mesh, in_specs=in_specs, out_specs=out_specs, check_vma=False
    )
```

```python
import jax
import jax.numpy as jnp
from jax import lax
from jax.sharding import PartitionSpec as P

VELOCITY = (
    (0, 0, 0),
    (1, 0, 0),
    (-1, 0, 0),
    (0, 1, 0),
    (0, -1, 0),
    (0, 0, 1),
    (0, 0, -1),
    (1, 1, 0),
    (-1, -1, 0),
    (1, -1, 0),
    (-1, 1, 0),
    (1, 0, 1),
    (-1, 0, -1),
    (1, 0, -1),
    (-1, 0, 1),
    (0, 1, 1),
    (0, -1, -1),
    (0, 1, -1),
    (0, -1, 1),
)
OPPOSITE = (0, 2, 1, 4, 3, 6, 5, 8, 7, 10, 9, 12, 11, 14, 13, 16, 15, 18, 17)
WEIGHTS = (1.0 / 3.0,) + (1.0 / 18.0,) * 6 + (1.0 / 36.0,) * 12
relaxation = 1.6
inlet_speed = 0.05
highest = lax.Precision.HIGHEST


def padded(block, sides, width):
    for axis, dim in sides:
        count = lax.axis_size(axis)
        forward = [(i, i + 1) for i in range(count - 1)]
        backward = [(target, source) for source, target in forward]
        low = lax.ppermute(
            lax.slice_in_dim(block, block.shape[dim] - width, None, axis=dim), axis, forward
        )
        high = lax.ppermute(lax.slice_in_dim(block, 0, width, axis=dim), axis, backward)
        block = jnp.concatenate([low, block, high], axis=dim)
    return block


def equilibrium(density, flow_x, flow_y, flow_z):
    square = flow_x * flow_x + flow_y * flow_y + flow_z * flow_z
    layers = []
    for component in range(19):
        step_x, step_y, step_z = VELOCITY[component]
        projection = step_x * flow_x + step_y * flow_y + step_z * flow_z
        layers.append(
            WEIGHTS[component]
            * density
            * (1.0 + 3.0 * projection + 4.5 * projection * projection - 1.5 * square)
        )
    return jnp.stack(layers)


def moment(populations, dimension):
    total = jnp.zeros_like(populations[0])
    for component in range(19):
        factor = VELOCITY[component][dimension]
        if factor != 0:
            total = total + factor * populations[component]
    return total


def collide(populations, porosity, node_kind):
    density = jnp.sum(populations, axis=0)
    flow_x = moment(populations, 0) / density
    flow_y = moment(populations, 1) / density
    flow_z = moment(populations, 2) / density
    retained = 1.0 - porosity
    fluid_post = populations - relaxation * (
        populations - equilibrium(density, retained * flow_x, retained * flow_y, retained * flow_z)
    )
    solid_post = jnp.stack([populations[OPPOSITE[component]] for component in range(19)])
    unit_density = jnp.ones_like(density)
    inlet_post = equilibrium(
        unit_density, inlet_speed * unit_density, jnp.zeros_like(density), jnp.zeros_like(density)
    )
    outlet_post = equilibrium(unit_density, flow_x, flow_y, flow_z)
    kind_here = node_kind[None]
    return jnp.where(
        kind_here == 0,
        fluid_post,
        jnp.where(kind_here == 1, solid_post, jnp.where(kind_here == 2, inlet_post, outlet_post)),
    )


def basis_matrix(fine_count, coarse_count, fine_offset, coarse_offset):
    fine_pos = jnp.arange(fine_count, dtype=jnp.float32) + fine_offset
    coarse_pos = jnp.arange(coarse_count, dtype=jnp.float32) + coarse_offset
    distance = fine_pos[:, None] - 4.0 * coarse_pos[None, :] - 1.5
    radius = jnp.abs(distance) / 6.0
    return jnp.where(radius < 1.0, (1.0 - radius) ** 4 * (1.0 + 4.0 * radius), 0.0)


def moving(dimension):
    return [component for component in range(19) if VELOCITY[component][dimension] != 0]


def pull_along(lane_list, dimension, extended):
    length_here = lane_list[0].shape[dimension]
    result = list(lane_list)
    for position, component in enumerate(moving(dimension)):
        offset = 1 + VELOCITY[component][dimension]
        result[component] = lax.slice_in_dim(
            extended[position], offset, offset + length_here, axis=dimension
        )
    return result


def fold_rim(bordered, dimension):
    length_here = bordered.shape[dimension]
    middle = lax.slice_in_dim(bordered, 2, length_here - 2, axis=dimension)
    head_slice = lax.slice_in_dim(bordered, 0, 1, axis=dimension)
    tail_slice = lax.slice_in_dim(bordered, length_here - 1, length_here, axis=dimension)
    middle_count = length_here - 4
    head_pads = [(0, 0)] * 3
    tail_pads = [(0, 0)] * 3
    head_pads[dimension] = (0, middle_count - 1)
    tail_pads[dimension] = (middle_count - 1, 0)
    return middle + jnp.pad(head_slice, head_pads) + jnp.pad(tail_slice, tail_pads)


def per_device(forward_pops, adjoint_pops, coefficients, node_kind):
    cells_x, cells_y, cells_z = node_kind.shape
    coarse_x, coarse_y, coarse_z = coefficients.shape
    window = padded(coefficients, (("gx", 0), ("gy", 1), ("gz", 2)), 1)
    basis_x = basis_matrix(cells_x, coarse_x + 2, 0, -1)
    basis_y = basis_matrix(cells_y, coarse_y + 2, 0, -1)
    basis_z = basis_matrix(cells_z, coarse_z + 2, 0, -1)
    partway = jnp.einsum("ijk,zk->ijz", window, basis_z, precision=highest)
    partway = jnp.einsum("ijz,yj->iyz", partway, basis_y, precision=highest)
    level_set = jnp.einsum("iyz,xi->xyz", partway, basis_x, precision=highest)
    bent = jnp.tanh(4.0 * level_set)
    porosity = 0.45 * (1.0 - bent)
    slope_phi = -1.8 * (1.0 - bent * bent)
    lane_list = [adjoint_pops[component] for component in range(19)]
    extended = padded(jnp.stack([lane_list[component] for component in moving(0)]), (("gx", 1),), 1)
    lane_list = pull_along(lane_list, 0, extended)
    extended = padded(jnp.stack([lane_list[component] for component in moving(1)]), (("gy", 2),), 1)
    lane_list = pull_along(lane_list, 1, extended)
    extended = padded(jnp.stack([lane_list[component] for component in moving(2)]), (("gz", 3),), 1)
    lane_list = pull_along(lane_list, 2, extended)
    pulled = jnp.stack(lane_list).astype(jnp.float32)
    forward = forward_pops.astype(jnp.float32)

    def local_collide(populations, porosity_here):
        return collide(populations, porosity_here, node_kind)

    unused, pullback = jax.vjp(local_collide, forward, porosity)
    prior, porosity_bar = pullback(pulled)
    prior_adjoint = prior.astype(jnp.bfloat16)
    sensitivity = porosity_bar * slope_phi
    partial_value = jnp.einsum("xyz,xi->iyz", sensitivity, basis_x, precision=highest)
    partial_value = jnp.einsum("iyz,yj->ijz", partial_value, basis_y, precision=highest)
    partial_value = jnp.einsum("ijz,zk->ijk", partial_value, basis_z, precision=highest)
    bordered = padded(partial_value, (("gz", 2), ("gy", 1), ("gx", 0)), 1)
    gradient = fold_rim(fold_rim(fold_rim(bordered, 0), 1), 2)
    return (prior_adjoint, gradient)


def solution(mesh):
    in_specs = (
        P(None, ("parts", "gx"), "gy", "gz"),
        P(None, ("parts", "gx"), "gy", "gz"),
        P(("parts", "gx"), "gy", "gz"),
        P(("parts", "gx"), "gy", "gz"),
    )
    out_specs = (P(None, ("parts", "gx"), "gy", "gz"), P(("parts", "gx"), "gy", "gz"))
    return jax.shard_map(
        per_device, mesh=mesh, in_specs=in_specs, out_specs=out_specs, check_vma=False
    )
```

```python
import jax
import jax.numpy as jnp
from jax import lax
from jax.sharding import PartitionSpec as P

VELOCITY = (
    (0, 0, 0),
    (1, 0, 0),
    (-1, 0, 0),
    (0, 1, 0),
    (0, -1, 0),
    (0, 0, 1),
    (0, 0, -1),
    (1, 1, 0),
    (-1, -1, 0),
    (1, -1, 0),
    (-1, 1, 0),
    (1, 0, 1),
    (-1, 0, -1),
    (1, 0, -1),
    (-1, 0, 1),
    (0, 1, 1),
    (0, -1, -1),
    (0, 1, -1),
    (0, -1, 1),
)
OPPOSITE = (0, 2, 1, 4, 3, 6, 5, 8, 7, 10, 9, 12, 11, 14, 13, 16, 15, 18, 17)
WEIGHTS = (1.0 / 3.0,) + (1.0 / 18.0,) * 6 + (1.0 / 36.0,) * 12
relaxation = 1.6
inlet_speed = 0.05
highest = lax.Precision.HIGHEST


def padded(block, sides, width):
    for axis, dim in sides:
        count = lax.axis_size(axis)
        forward = [(i, i + 1) for i in range(count - 1)]
        backward = [(target, source) for source, target in forward]
        low = lax.ppermute(
            lax.slice_in_dim(block, block.shape[dim] - width, None, axis=dim), axis, forward
        )
        high = lax.ppermute(lax.slice_in_dim(block, 0, width, axis=dim), axis, backward)
        block = jnp.concatenate([low, block, high], axis=dim)
    return block


def equilibrium(density, flow_x, flow_y, flow_z):
    square = flow_x * flow_x + flow_y * flow_y + flow_z * flow_z
    layers = []
    for component in range(19):
        step_x, step_y, step_z = VELOCITY[component]
        projection = step_x * flow_x + step_y * flow_y + step_z * flow_z
        layers.append(
            WEIGHTS[component]
            * density
            * (1.0 + 3.0 * projection + 4.5 * projection * projection - 1.5 * square)
        )
    return jnp.stack(layers)


def moment(populations, dimension):
    total = jnp.zeros_like(populations[0])
    for component in range(19):
        factor = VELOCITY[component][dimension]
        if factor != 0:
            total = total + factor * populations[component]
    return total


def collide(populations, porosity, node_kind):
    density = jnp.sum(populations, axis=0)
    flow_x = moment(populations, 0) / density
    flow_y = moment(populations, 1) / density
    flow_z = moment(populations, 2) / density
    retained = 1.0 - porosity
    fluid_post = populations - relaxation * (
        populations - equilibrium(density, retained * flow_x, retained * flow_y, retained * flow_z)
    )
    solid_post = jnp.stack([populations[OPPOSITE[component]] for component in range(19)])
    unit_density = jnp.ones_like(density)
    inlet_post = equilibrium(
        unit_density, inlet_speed * unit_density, jnp.zeros_like(density), jnp.zeros_like(density)
    )
    outlet_post = equilibrium(unit_density, flow_x, flow_y, flow_z)
    kind_here = node_kind[None]
    return jnp.where(
        kind_here == 0,
        fluid_post,
        jnp.where(kind_here == 1, solid_post, jnp.where(kind_here == 2, inlet_post, outlet_post)),
    )


def basis_matrix(fine_count, coarse_count, fine_offset, coarse_offset):
    fine_pos = jnp.arange(fine_count, dtype=jnp.float32) + fine_offset
    coarse_pos = jnp.arange(coarse_count, dtype=jnp.float32) + coarse_offset
    distance = fine_pos[:, None] - 4.0 * coarse_pos[None, :] - 1.5
    radius = jnp.abs(distance) / 6.0
    return jnp.where(radius < 1.0, (1.0 - radius) ** 4 * (1.0 + 4.0 * radius), 0.0)


def moving(dimension):
    return [component for component in range(19) if VELOCITY[component][dimension] != 0]


def pull_along(lane_list, dimension, extended):
    length_here = lane_list[0].shape[dimension]
    result = list(lane_list)
    for position, component in enumerate(moving(dimension)):
        offset = 1 + VELOCITY[component][dimension]
        result[component] = lax.slice_in_dim(
            extended[position], offset, offset + length_here, axis=dimension
        )
    return result


def fold_rim(bordered, dimension):
    length_here = bordered.shape[dimension]
    middle = lax.slice_in_dim(bordered, 2, length_here - 2, axis=dimension)
    head_slice = lax.slice_in_dim(bordered, 0, 1, axis=dimension)
    tail_slice = lax.slice_in_dim(bordered, length_here - 1, length_here, axis=dimension)
    middle_count = length_here - 4
    head_pads = [(0, 0)] * 3
    tail_pads = [(0, 0)] * 3
    head_pads[dimension] = (0, middle_count - 1)
    tail_pads[dimension] = (middle_count - 1, 0)
    return middle + jnp.pad(head_slice, head_pads) + jnp.pad(tail_slice, tail_pads)


def per_device(forward_pops, adjoint_pops, coefficients, node_kind):
    cells_x, cells_y, cells_z = node_kind.shape
    coarse_x, coarse_y, coarse_z = coefficients.shape
    window = padded(coefficients, (("gz", 2), ("gy", 1), ("gx", 0)), 1)
    basis_x = basis_matrix(cells_x, coarse_x + 2, 0, -1)
    basis_y = basis_matrix(cells_y, coarse_y + 2, 0, -1)
    basis_z = basis_matrix(cells_z, coarse_z + 2, 0, -1)
    partway = jnp.einsum("ijk,zk->ijz", window, basis_z, precision=highest)
    partway = jnp.einsum("ijz,yj->iyz", partway, basis_y, precision=highest)
    level_set = jnp.einsum("iyz,xi->xyz", partway, basis_x, precision=highest)
    bent = jnp.tanh(4.0 * level_set)
    porosity = 0.45 * (1.0 - bent)
    slope_phi = -1.8 * (1.0 - bent * bent)
    lane_list = [adjoint_pops[component] for component in range(19)]
    extended = padded(jnp.stack([lane_list[component] for component in moving(0)]), (("gx", 1),), 1)
    lane_list = pull_along(lane_list, 0, extended)
    extended = padded(jnp.stack([lane_list[component] for component in moving(1)]), (("gy", 2),), 1)
    lane_list = pull_along(lane_list, 1, extended)
    extended = padded(jnp.stack([lane_list[component] for component in moving(2)]), (("gz", 3),), 1)
    lane_list = pull_along(lane_list, 2, extended)
    pulled = jnp.stack(lane_list).astype(jnp.float32)
    forward = forward_pops.astype(jnp.float32)

    def local_collide(populations, porosity_here):
        return collide(populations, porosity_here, node_kind)

    unused, pullback = jax.vjp(local_collide, forward, porosity)
    prior, porosity_bar = pullback(pulled)
    prior_adjoint = prior.astype(jnp.bfloat16)
    sensitivity = porosity_bar * slope_phi
    partial_value = jnp.einsum("xyz,xi->iyz", sensitivity, basis_x, precision=highest)
    partial_value = jnp.einsum("iyz,yj->ijz", partial_value, basis_y, precision=highest)
    partial_value = jnp.einsum("ijz,zk->ijk", partial_value, basis_z, precision=highest)
    bordered = padded(partial_value, (("gz", 2), ("gy", 1), ("gx", 0)), 1)
    gradient = fold_rim(fold_rim(fold_rim(bordered, 0), 1), 2)
    return (prior_adjoint, gradient)


def solution(mesh):
    in_specs = (
        P(None, ("parts", "gx"), "gy", "gz"),
        P(None, ("parts", "gx"), "gy", "gz"),
        P(("parts", "gx"), "gy", "gz"),
        P(("parts", "gx"), "gy", "gz"),
    )
    out_specs = (P(None, ("parts", "gx"), "gy", "gz"), P(("parts", "gx"), "gy", "gz"))
    return jax.shard_map(
        per_device, mesh=mesh, in_specs=in_specs, out_specs=out_specs, check_vma=False
    )
```
